32 devices in a mesh: prow: 4 (over y, core), pcol: 8 (over z, x).
Axes of the slice: x: 2, y: 2, z: 4, core: 2. Of those that a mesh axis runs over, the one named last changes fastest.
Arguments:
- ainv_trail: float32 [2048, 2048], P('prow', 'pcol')
- panel_parent: float32 [2048, 256], P('prow', 'pcol'), may hold values from -0.125 to 0.125
- panel_child: float32 [2048, 256], P('prow', 'pcol'), may hold values from -0.125 to 0.125
- link_block: float32 [256, 256], replicated, may hold values from -0.375 to 0.375
- dinv_parent: float32 [256, 256], replicated
- dinv_child: float32 [256, 256], replicated
- pattern_parent: int32 [8], replicated, may hold values from 0 to 1, as said below
- pattern_child: int32 [8], replicated, may hold values from 0 to 1, as said below
Outputs:
- row_parent: float32 [256, 2048], P('prow', 'pcol')
- diag_parent: float32 [256, 256], P('prow')
- cross_child: float32 [256, 256], P('prow')
- row_child: float32 [256, 2048], P('prow', 'pcol')
- diag_child: float32 [256, 256], P('prow')
The draws below stay inside these ranges and needn't reach their ends.
Inputs may be any that keep to these rules, and one draw needn't show every extreme that they name: `pattern_parent`: each entry is 0 or 1; the first entry is 1 and at least one entry is 0. `pattern_child`: each entry is 0 or 1, and is 1 only where pattern_parent is 1; the first entry is 1.
All inputs are finite; a program needn't handle non-finite values.
Results may differ from the reference program's by a relative error of at most 0.00009.
Values sent between devices are 32-bit elements; how exact they have to be, the bound alone decides.
A program may use at most 64 MiB of HBM per device.

```python
import jax
import jax.numpy as jnp
from jax import lax

B = 256
NB = 8


def symmetric_draw(key, order):
    values = jax.random.normal(key, (order, order), jnp.float32)
    return (values + values.T) * 0.7071


def draw_ainv_trail(key, part):
    return symmetric_draw(jax.random.fold_in(key, 3), NB * B)


def draw_dinv_parent(key, part):
    return symmetric_draw(jax.random.fold_in(key, 5), B)


def draw_dinv_child(key, part):
    return symmetric_draw(jax.random.fold_in(key, 7), B)


def pattern_pair(key):
    base = jax.random.randint(jax.random.fold_in(key, 11), (NB,), 0, 4)
    extra = jax.random.randint(jax.random.fold_in(key, 13), (NB,), 0, 4)
    empty_slot = jax.random.randint(jax.random.fold_in(key, 17), (), 1, NB)
    base = base.at[0].set(3)
    base = base.at[empty_slot].set(0)
    extra = extra.at[0].set(3)
    parent = jnp.minimum(base, 1)
    child = parent * (extra // 2)
    return (parent.astype(jnp.int32), child.astype(jnp.int32))


def draw_pattern_parent(key, part):
    return pattern_pair(key)[0]


def draw_pattern_child(key, part):
    return pattern_pair(key)[1]


def shard_levels(rng, extent, split, least, largest):
    loudness = 1.0
    for position, parts in split:
        heights = jax.random.uniform(jax.random.fold_in(jax.random.fold_in(rng, 6), position), (parts,), jnp.float32, least / len(split), largest / len(split))
        loudness = loudness * jnp.repeat(jnp.exp(heights), extent[position] // parts).reshape((-1,) + (1,) * (len(extent) - 1 - position))
    return loudness


def noise(stream_key, extent, spread, limit, cuts=(), held_as=jnp.bfloat16):
    gain = shard_levels(stream_key, extent, cuts, -0.22, 0.18) if cuts else 1.0
    drawn = jax.random.normal(stream_key, extent, jnp.float32) * spread * gain
    return jnp.minimum(jnp.maximum(drawn, -limit), limit).astype(held_as)


def setup_inputs(seed: int = 0) -> dict:
    key_list = jax.random.split(jax.random.key(seed), 9)
    return {
        "ainv_trail": draw_ainv_trail(jax.random.fold_in(key_list[8], 71), 0),
        "panel_parent": noise(key_list[1], (NB * B, B), (NB * B) ** -0.5, 0.125, ((0, 4), (1, 8)), jnp.float32),
        "panel_child": noise(key_list[2], (NB * B, B), (NB * B) ** -0.5, 0.125, ((0, 4), (1, 8)), jnp.float32),
        "link_block": noise(key_list[3], (B, B), B ** -0.5, 0.375, (), jnp.float32),
        "dinv_parent": draw_dinv_parent(jax.random.fold_in(key_list[8], 71), 0),
        "dinv_child": draw_dinv_child(jax.random.fold_in(key_list[8], 71), 0),
        "pattern_parent": draw_pattern_parent(jax.random.fold_in(key_list[8], 71), 0),
        "pattern_child": draw_pattern_child(jax.random.fold_in(key_list[8], 71), 0),
    }


def lead_product(left, right):
    return lax.dot_general(left, right, (((0,), (0,)), ((), ())), precision=lax.Precision.HIGHEST, preferred_element_type=jnp.float32)


def plain_product(left, right):
    return jnp.dot(left, right, precision=lax.Precision.HIGHEST, preferred_element_type=jnp.float32)


def reference(ainv_trail, panel_parent, panel_child, link_block, dinv_parent, dinv_child, pattern_parent, pattern_child):
    parent_mask = jnp.repeat(pattern_parent.astype(jnp.float32), B)
    child_mask = jnp.repeat(pattern_child.astype(jnp.float32), B)
    parent_rows = panel_parent * parent_mask[:, None]
    child_rows = panel_child * child_mask[:, None]
    row_parent = -lead_product(parent_rows, ainv_trail) * parent_mask[None, :]
    diag_parent = dinv_parent - plain_product(row_parent, parent_rows)
    linked = plain_product(row_parent, child_rows)
    cross_child = -(lead_product(link_block, diag_parent) + linked.T)
    row_child = -(lead_product(child_rows, ainv_trail) + lead_product(link_block, row_parent)) * child_mask[None, :]
    diag_child = dinv_child - plain_product(cross_child, link_block) - plain_product(row_child, child_rows)
    return (row_parent, diag_parent, cross_child, row_child, diag_child)
```

```python
import functools

import jax
import jax.numpy as jnp
from jax import lax
from jax.experimental import pallas as pl
from jax.experimental.pallas import tpu as pltpu
from jax.sharding import PartitionSpec as P

MESH = pl.DeviceIdType.MESH

highest = lax.Precision.HIGHEST


def lead_product(left, right):
    return lax.dot_general(
        left, right, (((0,), (0,)), ((), ())), precision=highest, preferred_element_type=jnp.float32
    )


def plain_product(left, right):
    return jnp.dot(left, right, precision=highest, preferred_element_type=jnp.float32)


def block_mask(pattern, first, count, width):
    picked = lax.dynamic_slice(pattern, (first,), (count,)).astype(jnp.float32)
    return jnp.repeat(picked, width)


def row_total(partial_value, columns, row_index, share):
    total = lax.psum(partial_value, "prow")
    whole = -total * columns[None, :]
    return (lax.dynamic_slice_in_dim(whole, row_index * share, share, 0), whole)


def total_terms(stacked):
    return lax.psum(stacked, ("prow", "pcol"))


def column_terms(row_part, blocks):
    result = plain_product(row_part, blocks[0])
    return result


def on_device(
    ainv_trail,
    panel_parent,
    panel_child,
    link_block,
    dinv_parent,
    dinv_child,
    pattern_parent,
    pattern_child,
):
    width = link_block.shape[0]
    row_count = lax.axis_size("prow")
    row_index = lax.axis_index("prow")
    col_index = lax.axis_index("pcol")
    row_blocks = ainv_trail.shape[0] // width
    col_blocks = ainv_trail.shape[1] // width
    share = width // row_count
    first_row = row_index * row_blocks
    first_col = col_index * col_blocks
    parent_whole, child_whole = (
        lax.all_gather(panel_parent, "pcol", axis=1, tiled=True),
        lax.all_gather(panel_child, "pcol", axis=1, tiled=True),
    )
    parent_rows = parent_whole * block_mask(pattern_parent, first_row, row_blocks, width)[:, None]
    child_rows = child_whole * block_mask(pattern_child, first_row, row_blocks, width)[:, None]
    parent_cols = block_mask(pattern_parent, first_col, col_blocks, width)
    child_cols = block_mask(pattern_child, first_col, col_blocks, width)
    parent_partial = lead_product(parent_rows, ainv_trail)
    child_partial = lead_product(child_rows, ainv_trail)
    link_share = lax.dynamic_slice_in_dim(link_block, row_index * share, share, 0)
    block = first_col + 0
    root = block // row_blocks
    local = jnp.clip(block - first_row, 0, row_blocks - 1)
    parent_piece = lax.dynamic_slice_in_dim(parent_rows, local * width, width, 0)
    child_piece = lax.dynamic_slice_in_dim(child_rows, local * width, width, 0)
    owner = (root == row_index).astype(jnp.float32)
    parent_piece = parent_piece * owner
    child_piece = child_piece * owner
    parent_blocks = [parent_piece]
    child_blocks = [child_piece]
    parent_share, parent_part = row_total(parent_partial, parent_cols, row_index, share)
    first_terms = total_terms(
        jnp.stack(
            [column_terms(parent_part, parent_blocks), column_terms(parent_part, child_blocks)]
        )
    )
    diag_parent = dinv_parent - first_terms[0]
    cross_child = -(lead_product(link_block, diag_parent) + first_terms[1].T)
    child_partial = child_partial + lead_product(link_share, parent_share)
    child_share, child_part = row_total(child_partial, child_cols, row_index, share)
    second_terms = total_terms(jnp.stack([column_terms(child_part, child_blocks)]))
    diag_child = dinv_child - plain_product(cross_child, link_block) - second_terms[0]
    start = row_index * share
    return (
        parent_share,
        lax.dynamic_slice_in_dim(diag_parent, start, share, 0),
        lax.dynamic_slice_in_dim(cross_child, start, share, 0),
        child_share,
        lax.dynamic_slice_in_dim(diag_child, start, share, 0),
    )


def halves(value):
    high = value.astype(jnp.bfloat16)
    return high, (value - high.astype(jnp.float32)).astype(jnp.bfloat16)


def product(left, right, left_dim, right_dim):
    dims = (((left_dim,), (right_dim,)), ((), ()))
    (left_high, left_low), (right_high, right_low) = left, right

    def one(a, b):
        return lax.dot_general(a, b, dims, preferred_element_type=jnp.float32)

    return one(left_high, right_high) + (one(left_high, right_low) + one(left_low, right_high))


def kernel(
    rows,
    cols,
    pattern_parent,
    pattern_child,
    piece,
    ainv,
    link,
    dinv_parent,
    dinv_child,
    row_parent,
    diag_parent,
    cross_child,
    row_child,
    diag_child,
    panel,
    block_panel,
    ainv_high,
    ainv_low,
    masks,
    partial,
    arrived,
    terms,
    term_slots,
    finals,
    link_dinv,
    up_sem,
    down_sem,
    side_sem,
    panel_sem,
    own_sem,
    spread_sem,
    block_sem,
    share_send,
    share_recv,
    term_send,
    term_recv,
    final_send,
    final_recv,
):
    i, j = lax.axis_index("prow"), lax.axis_index("pcol")
    z, x = j // 2, j % 2
    depth = cols // 2
    width = link.shape[0]
    piece_rows = piece.shape[1]
    blocks = ainv.shape[0] // width
    share = width // rows
    own = share // cols
    other_x = 1 - x

    far = z // (depth // 2)
    near = z + far * (depth - 1 - 2 * z)
    steps = [near, 1 - near] + list(range(2, depth))
    levels = [s + far * (depth - 1 - 2 * s) for s in steps]

    def piece_of(level, side):
        start = pl.multiple_of((level * 2 + side) * piece_rows, piece_rows)
        return panel.at[:, pl.ds(start, piece_rows), :]

    def to(source, level, side, sem, device):
        return pltpu.make_async_remote_copy(
            src_ref=source,
            dst_ref=piece_of(level, side),
            send_sem=sem,
            recv_sem=panel_sem.at[level * 2 + side],
            device_id=device,
            device_id_type=MESH,
        )

    def up(source, level):
        return to(source, level, x, up_sem.at[level], (i, jnp.minimum(j + 2, cols - 1)))

    def down(source, level):
        return to(source, level, x, down_sem.at[level], (i, jnp.maximum(j - 2, 0)))

    def side(source, level):
        return to(source, level, x, side_sem.at[level], (i, z * 2 + other_x))

    def relay(source, level, act):
        @pl.when(jnp.logical_and(level <= z, z < depth - 1))
        def _():
            act(up(source, level))

        @pl.when(jnp.logical_and(level >= z, z > 0))
        def _():
            act(down(source, level))

        act(side(source, level))

    def start(copy):
        copy.start()

    owner = j // blocks
    half = pl.multiple_of((j % blocks) * width, width)

    def spread_copy(slot, k):
        begin = pl.multiple_of(slot * piece_rows, piece_rows)
        return pltpu.make_async_remote_copy(
            src_ref=panel.at[:, pl.ds(begin, piece_rows), pl.ds(half, width)],
            dst_ref=block_panel.at[:, pl.ds(begin, piece_rows), :],
            send_sem=spread_sem.at[slot, k],
            recv_sem=block_sem.at[slot],
            device_id=((i + 1 + k) % rows, j),
            device_id_type=MESH,
        )

    def keep_copy(slot):
        begin = pl.multiple_of(slot * piece_rows, piece_rows)
        return pltpu.make_async_copy(
            panel.at[:, pl.ds(begin, piece_rows), pl.ds(half, width)],
            block_panel.at[:, pl.ds(begin, piece_rows), :],
            block_sem.at[slot],
        )

    barrier = pltpu.get_barrier_semaphore()
    for k in range(1, cols):
        pl.semaphore_signal(barrier, inc=1, device_id=(i, (j + k) % cols), device_id_type=MESH)
    for k in range(1, rows):
        pl.semaphore_signal(barrier, inc=1, device_id=((i + k) % rows, j), device_id_type=MESH)
    keep_own = pltpu.make_async_copy(piece, piece_of(z, x), own_sem)
    keep_own.start()
    high, low = halves(ainv[...])
    ainv_high[...] = high
    ainv_low[...] = low
    for b in range(blocks):
        for p, pattern in enumerate((pattern_parent, pattern_child)):
            value = pattern[i * blocks + b].astype(jnp.float32)
            masks[p, :, b * width : (b + 1) * width] = jnp.full((piece_rows, width), 1.0, jnp.float32) * value
    pl.semaphore_wait(barrier, cols - 1 + rows - 1)
    relay(piece, z, start)

    def take(level, side_index):
        slot = level * 2 + side_index

        @pl.when(i == owner)
        def _():
            for k in range(rows - 1):
                spread_copy(slot, k).start()
            keep_copy(slot).start()

        begin = pl.multiple_of(slot * piece_rows, piece_rows)
        value = panel[:, pl.ds(begin, piece_rows), :] * masks[...]
        value = value.reshape(2 * piece_rows, value.shape[2])
        value_high, value_low = halves(value)
        both = jnp.concatenate([value_high, value_low], axis=0)
        first = jnp.dot(both, ainv_high[...], preferred_element_type=jnp.float32)
        second = jnp.dot(value_high, ainv_low[...], preferred_element_type=jnp.float32)
        total = first[: 2 * piece_rows] + first[2 * piece_rows :] + second
        partial[0, pl.ds(begin, piece_rows), :] = total[:piece_rows]
        partial[1, pl.ds(begin, piece_rows), :] = total[piece_rows:]

    link_halves = halves(link[...])
    link_dinv[...] = product(link_halves, halves(dinv_parent[...]), 0, 0)

    keep_own.wait()
    take(z, x)
    for k in range(1, depth + 1):
        if k < depth:
            level = levels[k]
            to(piece, level, x, own_sem, (i, z * 2 + other_x)).wait_recv()
            relay(piece_of(level, x), level, start)
            take(level, x)
        level = levels[k - 1]
        to(piece, level, other_x, own_sem, (i, z * 2 + other_x)).wait_recv()
        take(level, other_x)

    def share_copy(p, k):
        target = (i + k) % rows
        begin = pl.multiple_of(target * share, share)
        return pltpu.make_async_remote_copy(
            src_ref=partial.at[p, pl.ds(begin, share), :],
            dst_ref=arrived.at[p, k - 1],
            send_sem=share_send.at[p, k - 1],
            recv_sem=share_recv.at[p, k - 1],
            device_id=(target, j),
            device_id_type=MESH,
        )

    for k in (2, 1, 3):
        share_copy(0, k).start()
    partial[1] = partial[1] - product(link_halves, halves(partial[0]), 0, 0)
    for k in (2, 1, 3):
        share_copy(1, k).start()

    parent_here = pattern_parent[j].astype(jnp.float32)
    child_here = pattern_child[j].astype(jnp.float32)
    for slot in range(cols):
        keep_copy(slot).wait()
    parent_block = halves(block_panel[0])
    child_block = halves(block_panel[1])

    mine = pl.multiple_of(i * share, share)
    sums = []
    for p in range(2):
        total = partial[p, pl.ds(mine, share), :]
        for k in range(1, rows):
            share_copy(p, k).wait_recv()
            total = total + arrived[p, k - 1]
        sums.append(-total)
    parent_sum, child_sum = sums
    parent_sum = parent_sum * parent_here
    row_parent[...] = parent_sum
    row_child[...] = child_sum * child_here

    parent_terms = product(halves(jnp.concatenate([parent_sum, child_sum], axis=0)), parent_block, 1, 1)
    parent_terms = parent_terms * parent_here
    child_terms = product(halves(child_sum), child_block, 1, 1) * child_here
    terms[0] = parent_terms[:share]
    terms[1] = parent_terms[share:]
    terms[2] = child_terms

    def term_copy(k):
        target = (j + k) % cols
        begin = pl.multiple_of(target * own, own)
        return pltpu.make_async_remote_copy(
            src_ref=terms.at[:, pl.ds(begin, own), :],
            dst_ref=term_slots.at[k - 1],
            send_sem=term_send.at[k - 1],
            recv_sem=term_recv.at[k - 1],
            device_id=(i, target),
            device_id_type=MESH,
        )

    for k in range(1, cols):
        term_copy(k).start()
    begin = pl.multiple_of(j * own, own)
    place = pl.multiple_of(mine + begin, own)
    total = terms[:, pl.ds(begin, own), :]
    for k in range(1, cols):
        term_copy(k).wait_recv()
        total = total + term_slots[k - 1]
    cross = -(link_dinv[pl.ds(place, own), :] + total[1])
    finals[0, pl.ds(begin, own), :] = dinv_parent[pl.ds(place, own), :] - total[0]
    finals[1, pl.ds(begin, own), :] = cross
    finals[2, pl.ds(begin, own), :] = (
        dinv_child[pl.ds(place, own), :] - product(halves(cross), link_halves, 1, 0) - total[2]
    )

    def final_copy(k, origin):
        at = finals.at[:, pl.ds(pl.multiple_of(origin * own, own), own), :]
        return pltpu.make_async_remote_copy(
            src_ref=at,
            dst_ref=at,
            send_sem=final_send.at[k - 1],
            recv_sem=final_recv.at[k - 1],
            device_id=(i, (j + k) % cols),
            device_id_type=MESH,
        )

    for k in range(1, cols):
        final_copy(k, j).start()

    for k in range(depth):
        relay(piece_of(levels[k], x), levels[k], lambda copy: copy.wait_send())

    @pl.when(i == owner)
    def _():
        for slot in range(cols):
            for k in range(rows - 1):
                spread_copy(slot, k).wait_send()

    for p in range(2):
        for k in range(1, rows):
            share_copy(p, k).wait_send()
    for k in range(1, cols):
        term_copy(k).wait_send()
    for k in range(1, cols):
        final_copy(k, (j + cols - k) % cols).wait_recv()
    diag_parent[...] = finals[0]
    cross_child[...] = finals[1]
    diag_child[...] = finals[2]
    for k in range(1, cols):
        final_copy(k, j).wait_send()


def fused(rows, cols, ainv, parent, child, link, dinv_parent, dinv_child, pattern_parent, pattern_child):
    width = link.shape[0]
    share = width // rows
    own = share // cols
    piece = jnp.stack([parent.T, child.T])
    piece_rows, height = piece.shape[1:]
    f32 = jnp.float32
    dma = pltpu.SemaphoreType.DMA
    vmem = pl.BlockSpec(memory_space=pltpu.VMEM)
    smem = pl.BlockSpec(memory_space=pltpu.SMEM)
    wide = jax.ShapeDtypeStruct((share, width), f32)
    return pl.pallas_call(
        functools.partial(kernel, rows, cols),
        out_shape=(wide,) * 5,
        in_specs=[smem, smem] + [vmem] * 5,
        out_specs=(vmem,) * 5,
        scratch_shapes=[
            pltpu.VMEM((2, width, height), f32),
            pltpu.VMEM((2, width, width), f32),
            pltpu.VMEM((height, width), jnp.bfloat16),
            pltpu.VMEM((height, width), jnp.bfloat16),
            pltpu.VMEM((2, piece_rows, height), f32),
            pltpu.VMEM((2, width, width), f32),
            pltpu.VMEM((2, rows - 1, share, width), f32),
            pltpu.VMEM((3, share, width), f32),
            pltpu.VMEM((cols - 1, 3, own, width), f32),
            pltpu.VMEM((3, share, width), f32),
            pltpu.VMEM((width, width), f32),
            dma((cols // 2,)),
            dma((cols // 2,)),
            dma((cols // 2,)),
            dma((cols,)),
            dma,
            dma((cols, rows - 1)),
            dma((cols,)),
            dma((2, rows - 1)),
            dma((2, rows - 1)),
            dma((cols - 1,)),
            dma((cols - 1,)),
            dma((cols - 1,)),
            dma((cols - 1,)),
        ],
        compiler_params=pltpu.CompilerParams(collective_id=0, has_side_effects=True),
    )(pattern_parent, pattern_child, piece, ainv, link, dinv_parent, dinv_child)


def fits(rows, cols, width):
    return cols == 8 and width % (rows * cols * 8) == 0


def solution(mesh):
    rows, cols = mesh.shape["prow"], mesh.shape["pcol"]

    def step(ainv, parent, child, link, *rest):
        plain = ainv.shape[1] == link.shape[0] and parent.shape[1] % 8 == 0
        if plain and fits(rows, cols, link.shape[0]):
            return fused(rows, cols, ainv, parent, child, link, *rest)
        return on_device(ainv, parent, child, link, *rest)

    return jax.shard_map(
        step,
        mesh=mesh,
        in_specs=(P("prow", "pcol"), P("prow", "pcol"), P("prow", "pcol"), P(), P(), P(), P(), P()),
        out_specs=(
            P("prow", "pcol"),
            P("prow", None),
            P("prow", None),
            P("prow", "pcol"),
            P("prow", None),
        ),
        check_vma=False,
    )
```

```python
import functools

import jax
import jax.numpy as jnp
from jax import lax
from jax.experimental import pallas as pl
from jax.experimental.pallas import tpu as pltpu
from jax.sharding import PartitionSpec as P

MESH = pl.DeviceIdType.MESH

highest = lax.Precision.HIGHEST


def lead_product(left, right):
    return lax.dot_general(
        left, right, (((0,), (0,)), ((), ())), precision=highest, preferred_element_type=jnp.float32
    )


def plain_product(left, right):
    return jnp.dot(left, right, precision=highest, preferred_element_type=jnp.float32)


def block_mask(pattern, first, count, width):
    picked = lax.dynamic_slice(pattern, (first,), (count,)).astype(jnp.float32)
    return jnp.repeat(picked, width)


def row_total(partial_value, columns, row_index, share):
    total = lax.psum(partial_value, "prow")
    whole = -total * columns[None, :]
    return (lax.dynamic_slice_in_dim(whole, row_index * share, share, 0), whole)


def total_terms(stacked):
    return lax.psum(stacked, ("prow", "pcol"))


def column_terms(row_part, blocks):
    result = plain_product(row_part, blocks[0])
    return result


def on_device(
    ainv_trail,
    panel_parent,
    panel_child,
    link_block,
    dinv_parent,
    dinv_child,
    pattern_parent,
    pattern_child,
):
    width = link_block.shape[0]
    row_count = lax.axis_size("prow")
    row_index = lax.axis_index("prow")
    col_index = lax.axis_index("pcol")
    row_blocks = ainv_trail.shape[0] // width
    col_blocks = ainv_trail.shape[1] // width
    share = width // row_count
    first_row = row_index * row_blocks
    first_col = col_index * col_blocks
    parent_whole, child_whole = (
        lax.all_gather(panel_parent, "pcol", axis=1, tiled=True),
        lax.all_gather(panel_child, "pcol", axis=1, tiled=True),
    )
    parent_rows = parent_whole * block_mask(pattern_parent, first_row, row_blocks, width)[:, None]
    child_rows = child_whole * block_mask(pattern_child, first_row, row_blocks, width)[:, None]
    parent_cols = block_mask(pattern_parent, first_col, col_blocks, width)
    child_cols = block_mask(pattern_child, first_col, col_blocks, width)
    parent_partial = lead_product(parent_rows, ainv_trail)
    child_partial = lead_product(child_rows, ainv_trail)
    link_share = lax.dynamic_slice_in_dim(link_block, row_index * share, share, 0)
    block = first_col + 0
    root = block // row_blocks
    local = jnp.clip(block - first_row, 0, row_blocks - 1)
    parent_piece = lax.dynamic_slice_in_dim(parent_rows, local * width, width, 0)
    child_piece = lax.dynamic_slice_in_dim(child_rows, local * width, width, 0)
    owner = (root == row_index).astype(jnp.float32)
    parent_piece = parent_piece * owner
    child_piece = child_piece * owner
    parent_blocks = [parent_piece]
    child_blocks = [child_piece]
    parent_share, parent_part = row_total(parent_partial, parent_cols, row_index, share)
    first_terms = total_terms(
        jnp.stack(
            [column_terms(parent_part, parent_blocks), column_terms(parent_part, child_blocks)]
        )
    )
    diag_parent = dinv_parent - first_terms[0]
    cross_child = -(lead_product(link_block, diag_parent) + first_terms[1].T)
    child_partial = child_partial + lead_product(link_share, parent_share)
    child_share, child_part = row_total(child_partial, child_cols, row_index, share)
    second_terms = total_terms(jnp.stack([column_terms(child_part, child_blocks)]))
    diag_child = dinv_child - plain_product(cross_child, link_block) - second_terms[0]
    start = row_index * share
    return (
        parent_share,
        lax.dynamic_slice_in_dim(diag_parent, start, share, 0),
        lax.dynamic_slice_in_dim(cross_child, start, share, 0),
        child_share,
        lax.dynamic_slice_in_dim(diag_child, start, share, 0),
    )


def halves(value):
    high = value.astype(jnp.bfloat16)
    return high, (value - high.astype(jnp.float32)).astype(jnp.bfloat16)


def product(left, right, left_dim, right_dim):
    dims = (((left_dim,), (right_dim,)), ((), ()))
    (left_high, left_low), (right_high, right_low) = left, right

    def one(a, b):
        return lax.dot_general(a, b, dims, preferred_element_type=jnp.float32)

    return one(left_high, right_high) + (one(left_high, right_low) + one(left_low, right_high))


def kernel(
    rows,
    cols,
    pattern_parent,
    pattern_child,
    parent_in,
    child_in,
    ainv_in,
    link_in,
    dinv_parent_in,
    dinv_child_in,
    results,
    ainv,
    link,
    dinv_parent,
    dinv_child,
    panel,
    block_panel,
    ainv_high,
    ainv_low,
    masks,
    partial,
    arrived,
    terms,
    term_slots,
    finals,
    link_dinv,
    up_sem,
    down_sem,
    side_sem,
    panel_sem,
    own_sem,
    load_sem,
    spread_sem,
    block_sem,
    share_send,
    share_recv,
    term_send,
    term_recv,
    final_send,
    final_recv,
):
    i, j = lax.axis_index("prow"), lax.axis_index("pcol")
    z, x = j // 2, j % 2
    depth = cols // 2
    width = link.shape[0]
    piece_rows = parent_in.shape[0]
    blocks = ainv.shape[0] // width
    share = width // rows
    own = share // cols
    other_x = 1 - x

    far = z // (depth // 2)
    near = z + far * (depth - 1 - 2 * z)
    steps = [near, 1 - near] + list(range(2, depth))
    levels = [s + far * (depth - 1 - 2 * s) for s in steps]

    def piece_of(level, side):
        start = pl.multiple_of((level * 2 + side) * piece_rows, piece_rows)
        return panel.at[:, pl.ds(start, piece_rows), :]

    def to(source, level, side, sem, device):
        return pltpu.make_async_remote_copy(
            src_ref=source,
            dst_ref=piece_of(level, side),
            send_sem=sem,
            recv_sem=panel_sem.at[level * 2 + side],
            device_id=device,
            device_id_type=MESH,
        )

    def up(source, level):
        return to(source, level, x, up_sem.at[level], (i, jnp.minimum(j + 2, cols - 1)))

    def down(source, level):
        return to(source, level, x, down_sem.at[level], (i, jnp.maximum(j - 2, 0)))

    def side(source, level):
        return to(source, level, x, side_sem.at[level], (i, z * 2 + other_x))

    def relay(source, level, act):
        @pl.when(jnp.logical_and(level <= z, z < depth - 1))
        def _():
            act(up(source, level))

        @pl.when(jnp.logical_and(level >= z, z > 0))
        def _():
            act(down(source, level))

        act(side(source, level))

    def start(copy):
        copy.start()

    owner = j // blocks
    half = pl.multiple_of((j % blocks) * width, width)

    def spread_copy(slot, k):
        begin = pl.multiple_of(slot * piece_rows, piece_rows)
        return pltpu.make_async_remote_copy(
            src_ref=panel.at[:, pl.ds(begin, piece_rows), pl.ds(half, width)],
            dst_ref=block_panel.at[:, pl.ds(begin, piece_rows), :],
            send_sem=spread_sem.at[slot, k],
            recv_sem=block_sem.at[slot],
            device_id=((i + 1 + k) % rows, j),
            device_id_type=MESH,
        )

    def keep_copy(slot):
        begin = pl.multiple_of(slot * piece_rows, piece_rows)
        return pltpu.make_async_copy(
            panel.at[:, pl.ds(begin, piece_rows), pl.ds(half, width)],
            block_panel.at[:, pl.ds(begin, piece_rows), :],
            block_sem.at[slot],
        )

    barrier = pltpu.get_barrier_semaphore()
    for k in range(1, cols):
        pl.semaphore_signal(barrier, inc=1, device_id=(i, (j + k) % cols), device_id_type=MESH)
    for k in range(1, rows):
        pl.semaphore_signal(barrier, inc=1, device_id=((i + k) % rows, j), device_id_type=MESH)
    mine_at = pl.ds(pl.multiple_of(j * piece_rows, piece_rows), piece_rows)
    own_loads = [
        pltpu.make_async_copy(source, panel.at[p, mine_at, :], own_sem.at[p])
        for p, source in enumerate((parent_in, child_in))
    ]
    loads = [
        pltpu.make_async_copy(source, target, load_sem.at[n])
        for n, (source, target) in enumerate(
            (
                (ainv_in, ainv),
                (link_in, link),
                (dinv_parent_in, dinv_parent),
                (dinv_child_in, dinv_child),
            )
        )
    ]
    for load in own_loads + loads:
        load.start()
    for load in own_loads:
        load.wait()
    pl.semaphore_wait(barrier, cols - 1 + rows - 1)
    relay(piece_of(z, x), z, start)
    for load in loads:
        load.wait()
    high, low = halves(ainv[...])
    ainv_high[...] = high
    ainv_low[...] = low
    for b in range(blocks):
        for p, pattern in enumerate((pattern_parent, pattern_child)):
            value = pattern[i * blocks + b].astype(jnp.float32)
            masks[p, :, b * width : (b + 1) * width] = jnp.full((piece_rows, width), 1.0, jnp.float32) * value

    def take(level, side_index):
        slot = level * 2 + side_index

        @pl.when(i == owner)
        def _():
            for k in range(rows - 1):
                spread_copy(slot, k).start()
            keep_copy(slot).start()

        begin = pl.multiple_of(slot * piece_rows, piece_rows)
        value = panel[:, pl.ds(begin, piece_rows), :] * masks[...]
        value = value.reshape(2 * piece_rows, value.shape[2])
        value_high, value_low = halves(value)
        both = jnp.concatenate([value_high, value_low], axis=0)
        first = jnp.dot(both, ainv_high[...], preferred_element_type=jnp.float32)
        second = jnp.dot(value_high, ainv_low[...], preferred_element_type=jnp.float32)
        total = first[: 2 * piece_rows] + first[2 * piece_rows :] + second
        partial[0, pl.ds(begin, piece_rows), :] = total[:piece_rows]
        partial[1, pl.ds(begin, piece_rows), :] = total[piece_rows:]

    link_halves = halves(link[...])
    link_dinv[...] = product(link_halves, halves(dinv_parent[...]), 0, 0)

    take(z, x)
    for k in range(1, depth + 1):
        if k < depth:
            level = levels[k]
            to(piece_of(level, x), level, x, up_sem.at[0], (i, z * 2 + other_x)).wait_recv()
            relay(piece_of(level, x), level, start)
            take(level, x)
        level = levels[k - 1]
        to(piece_of(level, x), level, other_x, up_sem.at[0], (i, z * 2 + other_x)).wait_recv()
        take(level, other_x)

    def share_copy(p, k):
        target = (i + k) % rows
        begin = pl.multiple_of(target * share, share)
        return pltpu.make_async_remote_copy(
            src_ref=partial.at[p, pl.ds(begin, share), :],
            dst_ref=arrived.at[p, k - 1],
            send_sem=share_send.at[p, k - 1],
            recv_sem=share_recv.at[p, k - 1],
            device_id=(target, j),
            device_id_type=MESH,
        )

    for k in (2, 1, 3):
        share_copy(0, k).start()
    partial[1] = partial[1] - product(link_halves, halves(partial[0]), 0, 0)
    for k in (2, 1, 3):
        share_copy(1, k).start()

    parent_here = pattern_parent[j].astype(jnp.float32)
    child_here = pattern_child[j].astype(jnp.float32)
    for slot in range(cols):
        keep_copy(slot).wait()
    parent_block = halves(block_panel[0])
    child_block = halves(block_panel[1])

    mine = pl.multiple_of(i * share, share)
    sums = []
    for p in range(2):
        total = partial[p, pl.ds(mine, share), :]
        for k in range(1, rows):
            share_copy(p, k).wait_recv()
            total = total + arrived[p, k - 1]
        sums.append(-total)
    parent_sum, child_sum = sums
    parent_sum = parent_sum * parent_here
    results[0] = parent_sum
    results[3] = child_sum * child_here

    parent_terms = product(halves(jnp.concatenate([parent_sum, child_sum], axis=0)), parent_block, 1, 1)
    parent_terms = parent_terms * parent_here
    child_terms = product(halves(child_sum), child_block, 1, 1) * child_here
    terms[0] = parent_terms[:share]
    terms[1] = parent_terms[share:]
    terms[2] = child_terms

    def term_copy(k):
        target = (j + k) % cols
        begin = pl.multiple_of(target * own, own)
        return pltpu.make_async_remote_copy(
            src_ref=terms.at[:, pl.ds(begin, own), :],
            dst_ref=term_slots.at[k - 1],
            send_sem=term_send.at[k - 1],
            recv_sem=term_recv.at[k - 1],
            device_id=(i, target),
            device_id_type=MESH,
        )

    for k in range(1, cols):
        term_copy(k).start()
    begin = pl.multiple_of(j * own, own)
    place = pl.multiple_of(mine + begin, own)
    total = terms[:, pl.ds(begin, own), :]
    for k in range(1, cols):
        term_copy(k).wait_recv()
        total = total + term_slots[k - 1]
    cross = -(link_dinv[pl.ds(place, own), :] + total[1])
    finals[0, pl.ds(begin, own), :] = dinv_parent[pl.ds(place, own), :] - total[0]
    finals[1, pl.ds(begin, own), :] = cross
    finals[2, pl.ds(begin, own), :] = (
        dinv_child[pl.ds(place, own), :] - product(halves(cross), link_halves, 1, 0) - total[2]
    )

    def final_copy(k, origin):
        at = finals.at[:, pl.ds(pl.multiple_of(origin * own, own), own), :]
        return pltpu.make_async_remote_copy(
            src_ref=at,
            dst_ref=at,
            send_sem=final_send.at[k - 1],
            recv_sem=final_recv.at[k - 1],
            device_id=(i, (j + k) % cols),
            device_id_type=MESH,
        )

    for k in range(1, cols):
        final_copy(k, j).start()

    for k in range(depth):
        relay(piece_of(levels[k], x), levels[k], lambda copy: copy.wait_send())

    @pl.when(i == owner)
    def _():
        for slot in range(cols):
            for k in range(rows - 1):
                spread_copy(slot, k).wait_send()

    for p in range(2):
        for k in range(1, rows):
            share_copy(p, k).wait_send()
    for k in range(1, cols):
        term_copy(k).wait_send()
    for k in range(1, cols):
        final_copy(k, (j + cols - k) % cols).wait_recv()
    results[1] = finals[0]
    results[2] = finals[1]
    results[4] = finals[2]
    for k in range(1, cols):
        final_copy(k, j).wait_send()


def unpack(results, *outputs):
    for n, output in enumerate(outputs):
        output[...] = results[n]


def fused(rows, cols, ainv, parent, child, link, dinv_parent, dinv_child, pattern_parent, pattern_child):
    width = link.shape[0]
    share = width // rows
    own = share // cols
    height, piece_rows = parent.shape
    f32 = jnp.float32
    dma = pltpu.SemaphoreType.DMA
    vmem = pl.BlockSpec(memory_space=pltpu.VMEM)
    smem = pl.BlockSpec(memory_space=pltpu.SMEM)
    anywhere = pl.BlockSpec(memory_space=pl.ANY)
    wide = jax.ShapeDtypeStruct((share, width), f32)
    results = pl.pallas_call(
        functools.partial(kernel, rows, cols),
        out_shape=jax.ShapeDtypeStruct((5, share, width), f32),
        in_specs=[smem, smem] + [anywhere] * 6,
        out_specs=vmem,
        scratch_shapes=[
            pltpu.VMEM((height, width), f32),
            pltpu.VMEM((width, width), f32),
            pltpu.VMEM((width, width), f32),
            pltpu.VMEM((width, width), f32),
            pltpu.VMEM((2, width, height), f32),
            pltpu.VMEM((2, width, width), f32),
            pltpu.VMEM((height, width), jnp.bfloat16),
            pltpu.VMEM((height, width), jnp.bfloat16),
            pltpu.VMEM((2, piece_rows, height), f32),
            pltpu.VMEM((2, width, width), f32),
            pltpu.VMEM((2, rows - 1, share, width), f32),
            pltpu.VMEM((3, share, width), f32),
            pltpu.VMEM((cols - 1, 3, own, width), f32),
            pltpu.VMEM((3, share, width), f32),
            pltpu.VMEM((width, width), f32),
            dma((cols // 2,)),
            dma((cols // 2,)),
            dma((cols // 2,)),
            dma((cols,)),
            dma((2,)),
            dma((4,)),
            dma((cols, rows - 1)),
            dma((cols,)),
            dma((2, rows - 1)),
            dma((2, rows - 1)),
            dma((cols - 1,)),
            dma((cols - 1,)),
            dma((cols - 1,)),
            dma((cols - 1,)),
        ],
        compiler_params=pltpu.CompilerParams(collective_id=0, has_side_effects=True),
    )(pattern_parent, pattern_child, parent.T, child.T, ainv, link, dinv_parent, dinv_child)
    return pl.pallas_call(
        unpack,
        out_shape=(wide,) * 5,
        in_specs=[vmem],
        out_specs=(vmem,) * 5,
    )(results)


def fits(rows, cols, width):
    return cols == 8 and width % (rows * cols * 8) == 0


def solution(mesh):
    rows, cols = mesh.shape["prow"], mesh.shape["pcol"]

    def step(ainv, parent, child, link, *rest):
        plain = ainv.shape[1] == link.shape[0] and parent.shape[1] % 8 == 0
        if plain and fits(rows, cols, link.shape[0]):
            return fused(rows, cols, ainv, parent, child, link, *rest)
        return on_device(ainv, parent, child, link, *rest)

    return jax.shard_map(
        step,
        mesh=mesh,
        in_specs=(P("prow", "pcol"), P("prow", "pcol"), P("prow", "pcol"), P(), P(), P(), P(), P()),
        out_specs=(
            P("prow", "pcol"),
            P("prow", None),
            P("prow", None),
            P("prow", "pcol"),
            P("prow", None),
        ),
        check_vma=False,
    )
```

```python
import functools

import jax
import jax.numpy as jnp
from jax import lax
from jax.experimental import pallas as pl
from jax.experimental.pallas import tpu as pltpu
from jax.sharding import PartitionSpec as P

MESH = pl.DeviceIdType.MESH

highest = lax.Precision.HIGHEST


def lead_product(left, right):
    return lax.dot_general(
        left, right, (((0,), (0,)), ((), ())), precision=highest, preferred_element_type=jnp.float32
    )


def plain_product(left, right):
    return jnp.dot(left, right, precision=highest, preferred_element_type=jnp.float32)


def block_mask(pattern, first, count, width):
    picked = lax.dynamic_slice(pattern, (first,), (count,)).astype(jnp.float32)
    return jnp.repeat(picked, width)


def row_total(partial_value, columns, row_index, share):
    total = lax.psum(partial_value, "prow")
    whole = -total * columns[None, :]
    return (lax.dynamic_slice_in_dim(whole, row_index * share, share, 0), whole)


def total_terms(stacked):
    return lax.psum(stacked, ("prow", "pcol"))


def column_terms(row_part, blocks):
    result = plain_product(row_part, blocks[0])
    return result


def on_device(
    ainv_trail,
    panel_parent,
    panel_child,
    link_block,
    dinv_parent,
    dinv_child,
    pattern_parent,
    pattern_child,
):
    width = link_block.shape[0]
    row_count = lax.axis_size("prow")
    row_index = lax.axis_index("prow")
    col_index = lax.axis_index("pcol")
    row_blocks = ainv_trail.shape[0] // width
    col_blocks = ainv_trail.shape[1] // width
    share = width // row_count
    first_row = row_index * row_blocks
    first_col = col_index * col_blocks
    parent_whole, child_whole = (
        lax.all_gather(panel_parent, "pcol", axis=1, tiled=True),
        lax.all_gather(panel_child, "pcol", axis=1, tiled=True),
    )
    parent_rows = parent_whole * block_mask(pattern_parent, first_row, row_blocks, width)[:, None]
    child_rows = child_whole * block_mask(pattern_child, first_row, row_blocks, width)[:, None]
    parent_cols = block_mask(pattern_parent, first_col, col_blocks, width)
    child_cols = block_mask(pattern_child, first_col, col_blocks, width)
    parent_partial = lead_product(parent_rows, ainv_trail)
    child_partial = lead_product(child_rows, ainv_trail)
    link_share = lax.dynamic_slice_in_dim(link_block, row_index * share, share, 0)
    block = first_col + 0
    root = block // row_blocks
    local = jnp.clip(block - first_row, 0, row_blocks - 1)
    parent_piece = lax.dynamic_slice_in_dim(parent_rows, local * width, width, 0)
    child_piece = lax.dynamic_slice_in_dim(child_rows, local * width, width, 0)
    owner = (root == row_index).astype(jnp.float32)
    parent_piece = parent_piece * owner
    child_piece = child_piece * owner
    parent_blocks = [parent_piece]
    child_blocks = [child_piece]
    parent_share, parent_part = row_total(parent_partial, parent_cols, row_index, share)
    first_terms = total_terms(
        jnp.stack(
            [column_terms(parent_part, parent_blocks), column_terms(parent_part, child_blocks)]
        )
    )
    diag_parent = dinv_parent - first_terms[0]
    cross_child = -(lead_product(link_block, diag_parent) + first_terms[1].T)
    child_partial = child_partial + lead_product(link_share, parent_share)
    child_share, child_part = row_total(child_partial, child_cols, row_index, share)
    second_terms = total_terms(jnp.stack([column_terms(child_part, child_blocks)]))
    diag_child = dinv_child - plain_product(cross_child, link_block) - second_terms[0]
    start = row_index * share
    return (
        parent_share,
        lax.dynamic_slice_in_dim(diag_parent, start, share, 0),
        lax.dynamic_slice_in_dim(cross_child, start, share, 0),
        child_share,
        lax.dynamic_slice_in_dim(diag_child, start, share, 0),
    )


def halves(value):
    high = value.astype(jnp.bfloat16)
    return high, (value - high.astype(jnp.float32)).astype(jnp.bfloat16)


def product(left, right, left_dim, right_dim):
    dims = (((left_dim,), (right_dim,)), ((), ()))
    (left_high, left_low), (right_high, right_low) = left, right

    def one(a, b):
        return lax.dot_general(a, b, dims, preferred_element_type=jnp.float32)

    return one(left_high, right_high) + (one(left_high, right_low) + one(left_low, right_high))


def kernel(
    rows,
    cols,
    pattern_parent,
    pattern_child,
    parent_in,
    child_in,
    ainv_in,
    link_in,
    dinv_parent_in,
    dinv_child_in,
    results,
    ainv,
    link,
    dinv_parent,
    dinv_child,
    panel,
    block_panel,
    ainv_high,
    ainv_low,
    masks,
    partial,
    arrived,
    terms,
    term_slots,
    finals,
    link_dinv,
    up_sem,
    down_sem,
    side_sem,
    panel_sem,
    own_sem,
    load_sem,
    spread_sem,
    block_sem,
    share_send,
    share_recv,
    term_send,
    term_recv,
    final_send,
    final_recv,
):
    i, j = lax.axis_index("prow"), lax.axis_index("pcol")
    z, x = j // 2, j % 2
    depth = cols // 2
    width = link.shape[0]
    piece_rows = parent_in.shape[0]
    blocks = ainv.shape[0] // width
    share = width // rows
    own = share // cols
    other_x = 1 - x

    far = z // (depth // 2)
    near = z + far * (depth - 1 - 2 * z)
    steps = [near, 1 - near] + list(range(2, depth))
    levels = [s + far * (depth - 1 - 2 * s) for s in steps]

    def piece_of(level, side):
        start = pl.multiple_of((level * 2 + side) * piece_rows, piece_rows)
        return panel.at[:, pl.ds(start, piece_rows), :]

    def to(source, level, side, sem, device):
        return pltpu.make_async_remote_copy(
            src_ref=source,
            dst_ref=piece_of(level, side),
            send_sem=sem,
            recv_sem=panel_sem.at[level * 2 + side],
            device_id=device,
            device_id_type=MESH,
        )

    def up(source, level):
        return to(source, level, x, up_sem.at[level], (i, jnp.minimum(j + 2, cols - 1)))

    def down(source, level):
        return to(source, level, x, down_sem.at[level], (i, jnp.maximum(j - 2, 0)))

    def side(source, level):
        return to(source, level, x, side_sem.at[level], (i, z * 2 + other_x))

    def relay(source, level, act):
        @pl.when(jnp.logical_and(level <= z, z < depth - 1))
        def _():
            act(up(source, level))

        @pl.when(jnp.logical_and(level >= z, z > 0))
        def _():
            act(down(source, level))

        act(side(source, level))

    def start(copy):
        copy.start()

    owner = j // blocks
    half = pl.multiple_of((j % blocks) * width, width)

    across = (i + rows // 2) % rows
    mate = i + 1 - 2 * (i % 2)
    passes_on = across == owner

    def spread_copy(slot, k, passing=False):
        begin = pl.multiple_of(slot * piece_rows, piece_rows)
        landing = block_panel.at[:, pl.ds(begin, piece_rows), :]
        source = landing if passing else panel.at[:, pl.ds(begin, piece_rows), pl.ds(half, width)]
        return pltpu.make_async_remote_copy(
            src_ref=source,
            dst_ref=landing,
            send_sem=spread_sem.at[slot, k],
            recv_sem=block_sem.at[slot],
            device_id=((across, mate)[k], j),
            device_id_type=MESH,
        )

    def pass_on(slot):
        @pl.when(passes_on)
        def _():
            keep_copy(slot).wait()
            spread_copy(slot, 1, passing=True).start()

    def keep_copy(slot):
        begin = pl.multiple_of(slot * piece_rows, piece_rows)
        return pltpu.make_async_copy(
            panel.at[:, pl.ds(begin, piece_rows), pl.ds(half, width)],
            block_panel.at[:, pl.ds(begin, piece_rows), :],
            block_sem.at[slot],
        )

    barrier = pltpu.get_barrier_semaphore()
    for k in range(1, cols):
        pl.semaphore_signal(barrier, inc=1, device_id=(i, (j + k) % cols), device_id_type=MESH)
    for k in range(1, rows):
        pl.semaphore_signal(barrier, inc=1, device_id=((i + k) % rows, j), device_id_type=MESH)
    mine_at = pl.ds(pl.multiple_of(j * piece_rows, piece_rows), piece_rows)
    own_loads = [
        pltpu.make_async_copy(source, panel.at[p, mine_at, :], own_sem.at[p])
        for p, source in enumerate((parent_in, child_in))
    ]
    loads = [
        pltpu.make_async_copy(source, target, load_sem.at[n])
        for n, (source, target) in enumerate(
            (
                (ainv_in, ainv),
                (link_in, link),
                (dinv_parent_in, dinv_parent),
                (dinv_child_in, dinv_child),
            )
        )
    ]
    for load in own_loads + loads:
        load.start()
    for load in own_loads:
        load.wait()
    pl.semaphore_wait(barrier, cols - 1 + rows - 1)
    relay(piece_of(z, x), z, start)
    for load in loads:
        load.wait()
    high, low = halves(ainv[...])
    ainv_high[...] = high
    ainv_low[...] = low
    for b in range(blocks):
        for p, pattern in enumerate((pattern_parent, pattern_child)):
            value = pattern[i * blocks + b].astype(jnp.float32)
            masks[p, :, b * width : (b + 1) * width] = jnp.full((piece_rows, width), 1.0, jnp.float32) * value

    taken = []

    def take(level, side_index):
        slot = level * 2 + side_index
        taken.append(slot)

        @pl.when(i == owner)
        def _():
            for k in range(2):
                spread_copy(slot, k).start()
            keep_copy(slot).start()

        if len(taken) > 2:
            pass_on(taken[-3])

        begin = pl.multiple_of(slot * piece_rows, piece_rows)
        value = panel[:, pl.ds(begin, piece_rows), :] * masks[...]
        value = value.reshape(2 * piece_rows, value.shape[2])
        value_high, value_low = halves(value)
        both = jnp.concatenate([value_high, value_low], axis=0)
        first = jnp.dot(both, ainv_high[...], preferred_element_type=jnp.float32)
        second = jnp.dot(value_high, ainv_low[...], preferred_element_type=jnp.float32)
        total = first[: 2 * piece_rows] + first[2 * piece_rows :] + second
        partial[0, pl.ds(begin, piece_rows), :] = total[:piece_rows]
        partial[1, pl.ds(begin, piece_rows), :] = total[piece_rows:]

    link_halves = halves(link[...])
    link_dinv[...] = product(link_halves, halves(dinv_parent[...]), 0, 0)

    take(z, x)
    for k in range(1, depth + 1):
        if k < depth:
            level = levels[k]
            to(piece_of(level, x), level, x, up_sem.at[0], (i, z * 2 + other_x)).wait_recv()
            relay(piece_of(level, x), level, start)
            take(level, x)
        level = levels[k - 1]
        to(piece_of(level, x), level, other_x, up_sem.at[0], (i, z * 2 + other_x)).wait_recv()
        take(level, other_x)

    def share_copy(p, k):
        target = (i + k) % rows
        begin = pl.multiple_of(target * share, share)
        return pltpu.make_async_remote_copy(
            src_ref=partial.at[p, pl.ds(begin, share), :],
            dst_ref=arrived.at[p, k - 1],
            send_sem=share_send.at[p, k - 1],
            recv_sem=share_recv.at[p, k - 1],
            device_id=(target, j),
            device_id_type=MESH,
        )

    for k in (2, 1, 3):
        share_copy(0, k).start()
    partial[1] = partial[1] - product(link_halves, halves(partial[0]), 0, 0)
    for k in (2, 1, 3):
        share_copy(1, k).start()

    for slot in taken[-2:]:
        pass_on(slot)

    parent_here = pattern_parent[j].astype(jnp.float32)
    child_here = pattern_child[j].astype(jnp.float32)

    @pl.when(jnp.logical_not(passes_on))
    def _():
        for slot in range(cols):
            keep_copy(slot).wait()

    parent_block = halves(block_panel[0])
    child_block = halves(block_panel[1])
    mine = pl.multiple_of(i * share, share)
    begin = pl.multiple_of(j * own, own)
    place = pl.multiple_of(mine + begin, own)
    groups = ((0, 1), (1, 3))

    def share_total(p):
        total = partial[p, pl.ds(mine, share), :]
        for k in range(1, rows):
            share_copy(p, k).wait_recv()
            total = total + arrived[p, k - 1]
        return -total

    def term_copy(g, k):
        first, last = groups[g]
        target = (j + k) % cols
        at = pl.multiple_of(target * own, own)
        return pltpu.make_async_remote_copy(
            src_ref=terms.at[first:last, pl.ds(at, own), :],
            dst_ref=term_slots.at[k - 1, first:last],
            send_sem=term_send.at[g, k - 1],
            recv_sem=term_recv.at[g, k - 1],
            device_id=(i, target),
            device_id_type=MESH,
        )

    def term_total(g):
        first, last = groups[g]
        total = terms[first:last, pl.ds(begin, own), :]
        for k in range(1, cols):
            term_copy(g, k).wait_recv()
            total = total + term_slots[k - 1, first:last]
        return total

    def final_copy(g, k, origin):
        first, last = groups[g]
        at = finals.at[first:last, pl.ds(pl.multiple_of(origin * own, own), own), :]
        return pltpu.make_async_remote_copy(
            src_ref=at,
            dst_ref=at,
            send_sem=final_send.at[g, k - 1],
            recv_sem=final_recv.at[g, k - 1],
            device_id=(i, (j + k) % cols),
            device_id_type=MESH,
        )

    parent_sum = share_total(0) * parent_here
    terms[0] = product(halves(parent_sum), parent_block, 1, 1) * parent_here
    for k in range(1, cols):
        term_copy(0, k).start()
    results[0] = parent_sum
    child_sum = share_total(1)
    child_halves = halves(child_sum)
    terms[1] = product(child_halves, parent_block, 1, 1) * parent_here
    terms[2] = product(child_halves, child_block, 1, 1) * child_here
    for k in range(1, cols):
        term_copy(1, k).start()
    results[3] = child_sum * child_here

    finals[0, pl.ds(begin, own), :] = dinv_parent[pl.ds(place, own), :] - term_total(0)[0]
    for k in range(1, cols):
        final_copy(0, k, j).start()
    total = term_total(1)
    cross = -(link_dinv[pl.ds(place, own), :] + total[0])
    finals[1, pl.ds(begin, own), :] = cross
    finals[2, pl.ds(begin, own), :] = (
        dinv_child[pl.ds(place, own), :] - product(halves(cross), link_halves, 1, 0) - total[1]
    )
    for k in range(1, cols):
        final_copy(1, k, j).start()

    for k in range(depth):
        relay(piece_of(levels[k], x), levels[k], lambda copy: copy.wait_send())

    @pl.when(i == owner)
    def _():
        for slot in range(cols):
            for k in range(2):
                spread_copy(slot, k).wait_send()

    @pl.when(passes_on)
    def _():
        for slot in range(cols):
            spread_copy(slot, 1, passing=True).wait_send()

    for p in range(2):
        for k in range(1, rows):
            share_copy(p, k).wait_send()
    for g in range(2):
        for k in range(1, cols):
            term_copy(g, k).wait_send()
    for g in range(2):
        for k in range(1, cols):
            final_copy(g, k, (j + cols - k) % cols).wait_recv()
    for n, place_out in enumerate((1, 2, 4)):
        results[place_out] = finals[n]
    for g in range(2):
        for k in range(1, cols):
            final_copy(g, k, j).wait_send()


def unpack(results, *outputs):
    for n, output in enumerate(outputs):
        output[...] = results[n]


def fused(rows, cols, ainv, parent, child, link, dinv_parent, dinv_child, pattern_parent, pattern_child):
    width = link.shape[0]
    share = width // rows
    own = share // cols
    height, piece_rows = parent.shape
    f32 = jnp.float32
    dma = pltpu.SemaphoreType.DMA
    vmem = pl.BlockSpec(memory_space=pltpu.VMEM)
    smem = pl.BlockSpec(memory_space=pltpu.SMEM)
    anywhere = pl.BlockSpec(memory_space=pl.ANY)
    wide = jax.ShapeDtypeStruct((share, width), f32)
    results = pl.pallas_call(
        functools.partial(kernel, rows, cols),
        out_shape=jax.ShapeDtypeStruct((5, share, width), f32),
        in_specs=[smem, smem] + [anywhere] * 6,
        out_specs=vmem,
        scratch_shapes=[
            pltpu.VMEM((height, width), f32),
            pltpu.VMEM((width, width), f32),
            pltpu.VMEM((width, width), f32),
            pltpu.VMEM((width, width), f32),
            pltpu.VMEM((2, width, height), f32),
            pltpu.VMEM((2, width, width), f32),
            pltpu.VMEM((height, width), jnp.bfloat16),
            pltpu.VMEM((height, width), jnp.bfloat16),
            pltpu.VMEM((2, piece_rows, height), f32),
            pltpu.VMEM((2, width, width), f32),
            pltpu.VMEM((2, rows - 1, share, width), f32),
            pltpu.VMEM((3, share, width), f32),
            pltpu.VMEM((cols - 1, 3, own, width), f32),
            pltpu.VMEM((3, share, width), f32),
            pltpu.VMEM((width, width), f32),
            dma((cols // 2,)),
            dma((cols // 2,)),
            dma((cols // 2,)),
            dma((cols,)),
            dma((2,)),
            dma((4,)),
            dma((cols, 2)),
            dma((cols,)),
            dma((2, rows - 1)),
            dma((2, rows - 1)),
            dma((2, cols - 1)),
            dma((2, cols - 1)),
            dma((2, cols - 1)),
            dma((2, cols - 1)),
        ],
        compiler_params=pltpu.CompilerParams(collective_id=0, has_side_effects=True),
    )(pattern_parent, pattern_child, parent.T, child.T, ainv, link, dinv_parent, dinv_child)
    return pl.pallas_call(
        unpack,
        out_shape=(wide,) * 5,
        in_specs=[vmem],
        out_specs=(vmem,) * 5,
    )(results)


def fits(rows, cols, width):
    return rows == 4 and cols == 8 and width % (rows * cols * 8) == 0


def solution(mesh):
    rows, cols = mesh.shape["prow"], mesh.shape["pcol"]

    def step(ainv, parent, child, link, *rest):
        plain = ainv.shape[1] == link.shape[0] and parent.shape[1] % 8 == 0
        if plain and fits(rows, cols, link.shape[0]):
            return fused(rows, cols, ainv, parent, child, link, *rest)
        return on_device(ainv, parent, child, link, *rest)

    return jax.shard_map(
        step,
        mesh=mesh,
        in_specs=(P("prow", "pcol"), P("prow", "pcol"), P("prow", "pcol"), P(), P(), P(), P(), P()),
        out_specs=(
            P("prow", "pcol"),
            P("prow", None),
            P("prow", None),
            P("prow", "pcol"),
            P("prow", None),
        ),
        check_vma=False,
    )
```

```python
import functools

import jax
import jax.numpy as jnp
from jax import lax
from jax.experimental import pallas as pl
from jax.experimental.pallas import tpu as pltpu
from jax.sharding import PartitionSpec as P

MESH = pl.DeviceIdType.MESH

highest = lax.Precision.HIGHEST


def lead_product(left, right):
    return lax.dot_general(
        left, right, (((0,), (0,)), ((), ())), precision=highest, preferred_element_type=jnp.float32
    )


def plain_product(left, right):
    return jnp.dot(left, right, precision=highest, preferred_element_type=jnp.float32)


def block_mask(pattern, first, count, width):
    picked = lax.dynamic_slice(pattern, (first,), (count,)).astype(jnp.float32)
    return jnp.repeat(picked, width)


def row_total(partial_value, columns, row_index, share):
    total = lax.psum(partial_value, "prow")
    whole = -total * columns[None, :]
    return (lax.dynamic_slice_in_dim(whole, row_index * share, share, 0), whole)


def total_terms(stacked):
    return lax.psum(stacked, ("prow", "pcol"))


def column_terms(row_part, blocks):
    result = plain_product(row_part, blocks[0])
    return result


def on_device(
    ainv_trail,
    panel_parent,
    panel_child,
    link_block,
    dinv_parent,
    dinv_child,
    pattern_parent,
    pattern_child,
):
    width = link_block.shape[0]
    row_count = lax.axis_size("prow")
    row_index = lax.axis_index("prow")
    col_index = lax.axis_index("pcol")
    row_blocks = ainv_trail.shape[0] // width
    col_blocks = ainv_trail.shape[1] // width
    share = width // row_count
    first_row = row_index * row_blocks
    first_col = col_index * col_blocks
    parent_whole, child_whole = (
        lax.all_gather(panel_parent, "pcol", axis=1, tiled=True),
        lax.all_gather(panel_child, "pcol", axis=1, tiled=True),
    )
    parent_rows = parent_whole * block_mask(pattern_parent, first_row, row_blocks, width)[:, None]
    child_rows = child_whole * block_mask(pattern_child, first_row, row_blocks, width)[:, None]
    parent_cols = block_mask(pattern_parent, first_col, col_blocks, width)
    child_cols = block_mask(pattern_child, first_col, col_blocks, width)
    parent_partial = lead_product(parent_rows, ainv_trail)
    child_partial = lead_product(child_rows, ainv_trail)
    link_share = lax.dynamic_slice_in_dim(link_block, row_index * share, share, 0)
    block = first_col + 0
    root = block // row_blocks
    local = jnp.clip(block - first_row, 0, row_blocks - 1)
    parent_piece = lax.dynamic_slice_in_dim(parent_rows, local * width, width, 0)
    child_piece = lax.dynamic_slice_in_dim(child_rows, local * width, width, 0)
    owner = (root == row_index).astype(jnp.float32)
    parent_piece = parent_piece * owner
    child_piece = child_piece * owner
    parent_blocks = [parent_piece]
    child_blocks = [child_piece]
    parent_share, parent_part = row_total(parent_partial, parent_cols, row_index, share)
    first_terms = total_terms(
        jnp.stack(
            [column_terms(parent_part, parent_blocks), column_terms(parent_part, child_blocks)]
        )
    )
    diag_parent = dinv_parent - first_terms[0]
    cross_child = -(lead_product(link_block, diag_parent) + first_terms[1].T)
    child_partial = child_partial + lead_product(link_share, parent_share)
    child_share, child_part = row_total(child_partial, child_cols, row_index, share)
    second_terms = total_terms(jnp.stack([column_terms(child_part, child_blocks)]))
    diag_child = dinv_child - plain_product(cross_child, link_block) - second_terms[0]
    start = row_index * share
    return (
        parent_share,
        lax.dynamic_slice_in_dim(diag_parent, start, share, 0),
        lax.dynamic_slice_in_dim(cross_child, start, share, 0),
        child_share,
        lax.dynamic_slice_in_dim(diag_child, start, share, 0),
    )


def halves(value):
    high = value.astype(jnp.bfloat16)
    return high, (value - high.astype(jnp.float32)).astype(jnp.bfloat16)


def product(left, right, left_dim, right_dim):
    dims = (((left_dim,), (right_dim,)), ((), ()))
    (left_high, left_low), (right_high, right_low) = left, right

    def one(a, b):
        return lax.dot_general(a, b, dims, preferred_element_type=jnp.float32)

    return one(left_high, right_high) + (one(left_high, right_low) + one(left_low, right_high))


def kernel(
    rows,
    cols,
    pattern_parent,
    pattern_child,
    parent_in,
    child_in,
    ainv_in,
    link_in,
    dinv_parent_in,
    dinv_child_in,
    results,
    ainv,
    link,
    dinv_parent,
    dinv_child,
    panel,
    block_panel,
    ainv_high,
    ainv_low,
    masks,
    partial,
    arrived,
    terms,
    term_slots,
    finals,
    link_dinv,
    up_sem,
    down_sem,
    side_sem,
    panel_sem,
    own_sem,
    load_sem,
    spread_sem,
    block_sem,
    share_send,
    share_recv,
    term_send,
    term_recv,
    final_send,
    final_recv,
):
    i, j = lax.axis_index("prow"), lax.axis_index("pcol")
    z, x = j // 2, j % 2
    depth = cols // 2
    width = link.shape[0]
    piece_rows = parent_in.shape[0]
    blocks = ainv.shape[0] // width
    share = width // rows
    own = share // cols
    other_x = 1 - x

    far = z // (depth // 2)
    near = z + far * (depth - 1 - 2 * z)
    steps = [near, 1 - near] + list(range(2, depth))
    levels = [s + far * (depth - 1 - 2 * s) for s in steps]

    def piece_of(level, side):
        start = pl.multiple_of((level * 2 + side) * piece_rows, piece_rows)
        return panel.at[:, pl.ds(start, piece_rows), :]

    def to(source, level, side, sem, device):
        return pltpu.make_async_remote_copy(
            src_ref=source,
            dst_ref=piece_of(level, side),
            send_sem=sem,
            recv_sem=panel_sem.at[level * 2 + side],
            device_id=device,
            device_id_type=MESH,
        )

    def up(source, level):
        return to(source, level, x, up_sem.at[level], (i, jnp.minimum(j + 2, cols - 1)))

    def down(source, level):
        return to(source, level, x, down_sem.at[level], (i, jnp.maximum(j - 2, 0)))

    def side(source, level):
        return to(source, level, x, side_sem.at[level], (i, z * 2 + other_x))

    def relay(source, level, act):
        @pl.when(jnp.logical_and(level <= z, z < depth - 1))
        def _():
            act(up(source, level))

        @pl.when(jnp.logical_and(level >= z, z > 0))
        def _():
            act(down(source, level))

        act(side(source, level))

    def start(copy):
        copy.start()

    owner = j // blocks
    half = pl.multiple_of((j % blocks) * width, width)

    across = (i + rows // 2) % rows
    mate = i + 1 - 2 * (i % 2)
    passes_on = across == owner

    def spread_copy(slot, k, passing=False):
        begin = pl.multiple_of(slot * piece_rows, piece_rows)
        landing = block_panel.at[:, pl.ds(begin, piece_rows), :]
        source = landing if passing else panel.at[:, pl.ds(begin, piece_rows), pl.ds(half, width)]
        return pltpu.make_async_remote_copy(
            src_ref=source,
            dst_ref=landing,
            send_sem=spread_sem.at[slot, k],
            recv_sem=block_sem.at[slot],
            device_id=((across, mate)[k], j),
            device_id_type=MESH,
        )

    def pass_on(slot):
        @pl.when(passes_on)
        def _():
            keep_copy(slot).wait()
            spread_copy(slot, 1, passing=True).start()

    def keep_copy(slot):
        begin = pl.multiple_of(slot * piece_rows, piece_rows)
        return pltpu.make_async_copy(
            panel.at[:, pl.ds(begin, piece_rows), pl.ds(half, width)],
            block_panel.at[:, pl.ds(begin, piece_rows), :],
            block_sem.at[slot],
        )

    barrier = pltpu.get_barrier_semaphore()
    for k in range(1, cols):
        pl.semaphore_signal(barrier, inc=1, device_id=(i, (j + k) % cols), device_id_type=MESH)
    for k in range(1, rows):
        pl.semaphore_signal(barrier, inc=1, device_id=((i + k) % rows, j), device_id_type=MESH)
    mine_at = pl.ds(pl.multiple_of(j * piece_rows, piece_rows), piece_rows)
    own_loads = [
        pltpu.make_async_copy(source, panel.at[p, mine_at, :], own_sem.at[p])
        for p, source in enumerate((parent_in, child_in))
    ]
    loads = [
        pltpu.make_async_copy(source, target, load_sem.at[n])
        for n, (source, target) in enumerate(
            (
                (ainv_in, ainv),
                (link_in, link),
                (dinv_parent_in, dinv_parent),
                (dinv_child_in, dinv_child),
            )
        )
    ]
    for load in own_loads + loads:
        load.start()
    for load in own_loads:
        load.wait()
    pl.semaphore_wait(barrier, cols - 1 + rows - 1)
    relay(piece_of(z, x), z, start)
    for load in loads:
        load.wait()
    high, low = halves(ainv[...])
    ainv_high[...] = high
    ainv_low[...] = low
    for b in range(blocks):
        for p, pattern in enumerate((pattern_parent, pattern_child)):
            value = pattern[i * blocks + b].astype(jnp.float32)
            masks[p, :, b * width : (b + 1) * width] = jnp.full((piece_rows, width), 1.0, jnp.float32) * value

    taken = []

    def take(level, side_index):
        slot = level * 2 + side_index
        taken.append(slot)

        @pl.when(i == owner)
        def _():
            for k in range(2):
                spread_copy(slot, k).start()
            keep_copy(slot).start()

        if len(taken) > 2:
            pass_on(taken[-3])

        begin = pl.multiple_of(slot * piece_rows, piece_rows)
        value = panel[:, pl.ds(begin, piece_rows), :] * masks[...]
        value = value.reshape(2 * piece_rows, value.shape[2])
        value_high, value_low = halves(value)
        both = jnp.concatenate([value_high, value_low], axis=0)
        first = jnp.dot(both, ainv_high[...], preferred_element_type=jnp.float32)
        second = jnp.dot(value_high, ainv_low[...], preferred_element_type=jnp.float32)
        total = first[: 2 * piece_rows] + first[2 * piece_rows :] + second
        partial[0, pl.ds(begin, piece_rows), :] = total[:piece_rows]
        partial[1, pl.ds(begin, piece_rows), :] = total[piece_rows:]

    link_halves = halves(link[...])
    link_dinv[...] = product(link_halves, halves(dinv_parent[...]), 0, 0)

    take(z, x)
    for k in range(1, depth + 1):
        if k < depth:
            level = levels[k]
            to(piece_of(level, x), level, x, up_sem.at[0], (i, z * 2 + other_x)).wait_recv()
            relay(piece_of(level, x), level, start)
            take(level, x)
        level = levels[k - 1]
        to(piece_of(level, x), level, other_x, up_sem.at[0], (i, z * 2 + other_x)).wait_recv()
        take(level, other_x)

    def rows_of(device):
        return pl.ds(pl.multiple_of(device * share, share), share)

    def share_copy(p, n):
        source = ((mate + rows // 2) % rows, mate, across)[n]
        return pltpu.make_async_remote_copy(
            src_ref=partial.at[p, rows_of(source), :],
            dst_ref=arrived.at[p, n],
            send_sem=share_send.at[p, n],
            recv_sem=share_recv.at[p, n],
            device_id=((mate, mate, across)[n], j),
            device_id_type=MESH,
        )

    def cross_over(p):
        share_copy(p, 0).wait_recv()
        partial[p, rows_of(across), :] = partial[p, rows_of(across), :] + arrived[p, 0]
        share_copy(p, 2).start()

    for n in range(2):
        share_copy(0, n).start()
    partial[1] = partial[1] - product(link_halves, halves(partial[0]), 0, 0)
    for n in range(2):
        share_copy(1, n).start()
    for p in range(2):
        cross_over(p)
    for slot in taken[-2:]:
        pass_on(slot)

    parent_here = pattern_parent[j].astype(jnp.float32)
    child_here = pattern_child[j].astype(jnp.float32)

    @pl.when(jnp.logical_not(passes_on))
    def _():
        for slot in range(cols):
            keep_copy(slot).wait()

    parent_block = halves(block_panel[0])
    child_block = halves(block_panel[1])
    mine = pl.multiple_of(i * share, share)
    begin = pl.multiple_of(j * own, own)
    place = pl.multiple_of(mine + begin, own)
    groups = ((0, 1), (1, 3))

    def share_total(p):
        total = partial[p, pl.ds(mine, share), :]
        for n in range(1, rows - 1):
            share_copy(p, n).wait_recv()
            total = total + arrived[p, n]
        return -total

    def term_copy(g, k):
        first, last = groups[g]
        target = (j + k) % cols
        at = pl.multiple_of(target * own, own)
        return pltpu.make_async_remote_copy(
            src_ref=terms.at[first:last, pl.ds(at, own), :],
            dst_ref=term_slots.at[k - 1, first:last],
            send_sem=term_send.at[g, k - 1],
            recv_sem=term_recv.at[g, k - 1],
            device_id=(i, target),
            device_id_type=MESH,
        )

    def term_total(g):
        first, last = groups[g]
        total = terms[first:last, pl.ds(begin, own), :]
        for k in range(1, cols):
            term_copy(g, k).wait_recv()
            total = total + term_slots[k - 1, first:last]
        return total

    def final_copy(g, k, origin):
        first, last = groups[g]
        at = finals.at[first:last, pl.ds(pl.multiple_of(origin * own, own), own), :]
        return pltpu.make_async_remote_copy(
            src_ref=at,
            dst_ref=at,
            send_sem=final_send.at[g, k - 1],
            recv_sem=final_recv.at[g, k - 1],
            device_id=(i, (j + k) % cols),
            device_id_type=MESH,
        )

    parent_sum = share_total(0) * parent_here
    terms[0] = product(halves(parent_sum), parent_block, 1, 1) * parent_here
    for k in range(1, cols):
        term_copy(0, k).start()
    results[0] = parent_sum
    child_sum = share_total(1)
    child_halves = halves(child_sum)
    terms[1] = product(child_halves, parent_block, 1, 1) * parent_here
    terms[2] = product(child_halves, child_block, 1, 1) * child_here
    for k in range(1, cols):
        term_copy(1, k).start()
    results[3] = child_sum * child_here

    finals[0, pl.ds(begin, own), :] = dinv_parent[pl.ds(place, own), :] - term_total(0)[0]
    for k in range(1, cols):
        final_copy(0, k, j).start()
    total = term_total(1)
    cross = -(link_dinv[pl.ds(place, own), :] + total[0])
    finals[1, pl.ds(begin, own), :] = cross
    finals[2, pl.ds(begin, own), :] = (
        dinv_child[pl.ds(place, own), :] - product(halves(cross), link_halves, 1, 0) - total[1]
    )
    for k in range(1, cols):
        final_copy(1, k, j).start()

    for k in range(depth):
        relay(piece_of(levels[k], x), levels[k], lambda copy: copy.wait_send())

    @pl.when(i == owner)
    def _():
        for slot in range(cols):
            for k in range(2):
                spread_copy(slot, k).wait_send()

    @pl.when(passes_on)
    def _():
        for slot in range(cols):
            spread_copy(slot, 1, passing=True).wait_send()

    for p in range(2):
        for n in range(rows - 1):
            share_copy(p, n).wait_send()
    for g in range(2):
        for k in range(1, cols):
            term_copy(g, k).wait_send()
    for g in range(2):
        for k in range(1, cols):
            final_copy(g, k, (j + cols - k) % cols).wait_recv()
    for n, place_out in enumerate((1, 2, 4)):
        results[place_out] = finals[n]
    for g in range(2):
        for k in range(1, cols):
            final_copy(g, k, j).wait_send()


def unpack(results, *outputs):
    for n, output in enumerate(outputs):
        output[...] = results[n]


def fused(rows, cols, ainv, parent, child, link, dinv_parent, dinv_child, pattern_parent, pattern_child):
    width = link.shape[0]
    share = width // rows
    own = share // cols
    height, piece_rows = parent.shape
    f32 = jnp.float32
    dma = pltpu.SemaphoreType.DMA
    vmem = pl.BlockSpec(memory_space=pltpu.VMEM)
    smem = pl.BlockSpec(memory_space=pltpu.SMEM)
    anywhere = pl.BlockSpec(memory_space=pl.ANY)
    wide = jax.ShapeDtypeStruct((share, width), f32)
    results = pl.pallas_call(
        functools.partial(kernel, rows, cols),
        out_shape=jax.ShapeDtypeStruct((5, share, width), f32),
        in_specs=[smem, smem] + [anywhere] * 6,
        out_specs=vmem,
        scratch_shapes=[
            pltpu.VMEM((height, width), f32),
            pltpu.VMEM((width, width), f32),
            pltpu.VMEM((width, width), f32),
            pltpu.VMEM((width, width), f32),
            pltpu.VMEM((2, width, height), f32),
            pltpu.VMEM((2, width, width), f32),
            pltpu.VMEM((height, width), jnp.bfloat16),
            pltpu.VMEM((height, width), jnp.bfloat16),
            pltpu.VMEM((2, piece_rows, height), f32),
            pltpu.VMEM((2, width, width), f32),
            pltpu.VMEM((2, rows - 1, share, width), f32),
            pltpu.VMEM((3, share, width), f32),
            pltpu.VMEM((cols - 1, 3, own, width), f32),
            pltpu.VMEM((3, share, width), f32),
            pltpu.VMEM((width, width), f32),
            dma((cols // 2,)),
            dma((cols // 2,)),
            dma((cols // 2,)),
            dma((cols,)),
            dma((2,)),
            dma((4,)),
            dma((cols, 2)),
            dma((cols,)),
            dma((2, rows - 1)),
            dma((2, rows - 1)),
            dma((2, cols - 1)),
            dma((2, cols - 1)),
            dma((2, cols - 1)),
            dma((2, cols - 1)),
        ],
        compiler_params=pltpu.CompilerParams(collective_id=0, has_side_effects=True),
    )(pattern_parent, pattern_child, parent.T, child.T, ainv, link, dinv_parent, dinv_child)
    return pl.pallas_call(
        unpack,
        out_shape=(wide,) * 5,
        in_specs=[vmem],
        out_specs=(vmem,) * 5,
    )(results)


def fits(rows, cols, width):
    return rows == 4 and cols == 8 and width % (rows * cols * 8) == 0


def solution(mesh):
    rows, cols = mesh.shape["prow"], mesh.shape["pcol"]

    def step(ainv, parent, child, link, *rest):
        plain = ainv.shape[1] == link.shape[0] and parent.shape[1] % 8 == 0
        if plain and fits(rows, cols, link.shape[0]):
            return fused(rows, cols, ainv, parent, child, link, *rest)
        return on_device(ainv, parent, child, link, *rest)

    return jax.shard_map(
        step,
        mesh=mesh,
        in_specs=(P("prow", "pcol"), P("prow", "pcol"), P("prow", "pcol"), P(), P(), P(), P(), P()),
        out_specs=(
            P("prow", "pcol"),
            P("prow", None),
            P("prow", None),
            P("prow", "pcol"),
            P("prow", None),
        ),
        check_vma=False,
    )
```
